32 devices in a mesh: mem: 4 (over z), lat: 8 (over y, x, core).
Axes of the slice: x: 2, y: 2, z: 4, core: 2. Of those that a mesh axis runs over, the one named last changes fastest.
Arguments:
- features: bfloat16 [16, 16, 1440, 128], P('mem', 'lat'), may hold values from -6 to 6
- conv_inner: bfloat16 [3, 3, 128, 128], replicated, may hold values from -0.1875 to 0.1875
- conv_head: bfloat16 [3, 3, 128, 69], replicated, may hold values from -0.1875 to 0.1875
- truth: float32 [69, 16, 1440], P(None, 'lat'), may hold values from -5 to 5
- kernel_width: float32 [69], replicated, may hold values from 0.3 to 1.5
- var_weight: float32 [69], replicated, may hold values from 0.5 to 2
Outputs:
- grad_features: bfloat16 [16, 16, 1440, 128], P('mem', 'lat')
- grad_inner: float32 [3, 3, 128, 128], replicated
- grad_head: float32 [3, 3, 128, 69], replicated
The draws below stay inside these ranges and needn't reach their ends.
All inputs are finite; a program needn't handle non-finite values.
Results may differ from the reference program's by a relative error of at most 0.0098.
Values may be sent and summed in bfloat16 or wider, within the bound.
No kernel may reach another device: no remote copies, remote signals or barrier semaphores. Data moves between devices by JAX's collectives and lax.ppermute only.
A program may use at most 256 MiB of HBM per device.

```python
import math
import jax
import jax.numpy as jnp
from jax import lax

C = 128
V = 69
LON = 1440
MEMBERS = 16
NLAT = 16


def block_scale(key, shape, pieces, smallest, high):
    factor_of, own = 1.0, jax.random.fold_in(key, 6)
    for axis_at, parts in pieces:
        steps = jnp.exp(jax.random.uniform(jax.random.fold_in(own, axis_at), (parts,), jnp.float32, smallest / len(pieces), high / len(pieces)))
        factor_of = factor_of * jnp.repeat(steps, shape[axis_at] // parts).reshape([-1 if axis == axis_at else 1 for axis in range(len(shape))])
    return factor_of


def scatter_about(own_key, dims, scale, limit, shards=(), kind=jnp.bfloat16):
    level = block_scale(own_key, dims, shards, -0.22, 0.18) if shards else 1.0
    array = jax.random.normal(own_key, dims, jnp.float32) * scale * level
    return jnp.minimum(jnp.maximum(array, -limit), limit).astype(kind)


def setup_inputs(seed: int = 0) -> dict:
    key_of = jax.random.split(jax.random.key(seed), 7)
    return {
        "features": scatter_about(key_of[0], (MEMBERS, NLAT, LON, C), 1.0, 6.0, ((0, 4), (1, 8))),
        "conv_inner": scatter_about(key_of[1], (3, 3, C, C), (9 * C) ** -0.5, 0.1875),
        "conv_head": scatter_about(key_of[2], (3, 3, C, V), (9 * C) ** -0.5, 0.1875),
        "truth": scatter_about(key_of[3], (V, NLAT, LON), 0.7, 5.0, ((1, 8),), jnp.float32),
        "kernel_width": jnp.clip(jnp.exp(jax.random.uniform(key_of[4], (V,), jnp.float32, math.log(0.3), math.log(1.5))), 0.3, 1.5),
        "var_weight": jnp.clip(jnp.exp(jax.random.uniform(key_of[5], (V,), jnp.float32, math.log(0.5), math.log(2.0))), 0.5, 2.0),
    }


def wrap_lon(values, axis):
    count = values.shape[axis]
    return jnp.concatenate([lax.slice_in_dim(values, count - 1, count, axis=axis), values, lax.slice_in_dim(values, 0, 1, axis=axis)], axis=axis)


def pad_rows(values, axis):
    widths = [(0, 0)] * values.ndim
    widths[axis] = (1, 1)
    return jnp.pad(values, widths)


def gelu_slope(pre):
    return jax.jvp(jax.nn.gelu, (pre,), (jnp.ones_like(pre),))[1]


def reference(features, conv_inner, conv_head, truth, kernel_width, var_weight):
    inner32 = conv_inner.astype(jnp.float32)
    head32 = conv_head.astype(jnp.float32)

    def forward(member):
        feature_pad = wrap_lon(pad_rows(member, 0), 1).astype(jnp.float32)
        pre = jnp.zeros((NLAT, LON, C), jnp.float32)
        for row_off in range(3):
            for col_off in range(3):
                pre = pre + jnp.einsum("rlc,co->rlo", feature_pad[row_off:row_off + NLAT, col_off:col_off + LON], inner32[row_off, col_off])
        hidden = jax.nn.gelu(pre).astype(jnp.bfloat16)
        hidden_pad = wrap_lon(pad_rows(hidden, 0), 1).astype(jnp.float32)
        field = jnp.zeros((V, NLAT, LON), jnp.float32)
        for row_off in range(3):
            for col_off in range(3):
                field = field + jnp.einsum("rlc,cv->vrl", hidden_pad[row_off:row_off + NLAT, col_off:col_off + LON], head32[row_off, col_off])
        return pre, hidden, field.astype(jnp.bfloat16)

    pres, hiddens, fields = lax.map(forward, features)
    members = features.shape[0]
    inverse = 1.0 / (kernel_width * kernel_width)
    values = fields.astype(jnp.float32)

    def variable_pairs(packed):
        member_values, rate = packed
        spread = member_values[None] - member_values[:, None]
        kernel = jnp.exp(-0.5 * spread * spread * rate)
        return jnp.sum(kernel * spread, axis=1)

    pairwise = lax.map(variable_pairs, (jnp.moveaxis(values, 1, 0), inverse))
    pairwise = jnp.moveaxis(pairwise, 0, 1)
    offset = values - truth[None]
    nearness = jnp.exp(-0.5 * offset * offset * inverse[None, :, None, None])
    scale = (var_weight * inverse)[None, :, None, None]
    field_grad = (scale * ((2.0 / (members - 1)) * pairwise + 2.0 * nearness * offset)).astype(jnp.bfloat16)

    def backward(packed):
        member, pre, hidden, grad_field = packed
        feature_pad = wrap_lon(pad_rows(member, 0), 1).astype(jnp.float32)
        hidden_pad = wrap_lon(pad_rows(hidden, 0), 1).astype(jnp.float32)
        grad_pad = wrap_lon(pad_rows(grad_field, 1), 2).astype(jnp.float32)
        grad_values = grad_field.astype(jnp.float32)
        summed = jnp.zeros((NLAT, LON, C), jnp.float32)
        head_parts = []
        for row_off in range(3):
            for col_off in range(3):
                summed = summed + jnp.einsum("vrl,cv->rlc", grad_pad[:, 2 - row_off:2 - row_off + NLAT, 2 - col_off:2 - col_off + LON], head32[row_off, col_off])
                head_parts.append(jnp.einsum("rlc,vrl->cv", hidden_pad[row_off:row_off + NLAT, col_off:col_off + LON], grad_values))
        hidden_grad = (summed * gelu_slope(pre)).astype(jnp.bfloat16)
        dpad = wrap_lon(pad_rows(hidden_grad, 0), 1).astype(jnp.float32)
        hidden_values = hidden_grad.astype(jnp.float32)
        feature_grad = jnp.zeros((NLAT, LON, C), jnp.float32)
        inner_parts = []
        for row_off in range(3):
            for col_off in range(3):
                feature_grad = feature_grad + jnp.einsum("rlo,co->rlc", dpad[2 - row_off:2 - row_off + NLAT, 2 - col_off:2 - col_off + LON], inner32[row_off, col_off])
                inner_parts.append(jnp.einsum("rlc,rlo->co", feature_pad[row_off:row_off + NLAT, col_off:col_off + LON], hidden_values))
        inner_grad = jnp.stack(inner_parts).reshape((3, 3, C, C))
        head_grad = jnp.stack(head_parts).reshape((3, 3, C, V))
        return feature_grad.astype(jnp.bfloat16), inner_grad, head_grad

    grad_features, inner_all, head_all = lax.map(backward, (features, pres, hiddens, field_grad))
    points = NLAT * LON
    return grad_features, jnp.sum(inner_all, axis=0) / points, jnp.sum(head_all, axis=0) / points
```

```python
import functools
import math

import jax
import jax.numpy as jnp
from jax import lax
from jax.experimental import pallas as pl
from jax.experimental.pallas import tpu as pltpu
from jax.sharding import PartitionSpec as P

BF16 = jnp.bfloat16
F32 = jnp.float32
LANES = 128
EDGE = 8
VMEM_LIMIT = 60 * 1024 * 1024


def tile_of(count, step, most):
    return max(t for t in range(step, most + 1, step) if count % t == 0)


def shifted(ref, start, tile, first, count, offsets=(-1, 0, 1)):
    window = ref[pl.ds(start, tile + 2 * EDGE), first : first + count]
    return jnp.concatenate(
        [window[EDGE + off : EDGE + off + tile].astype(BF16) for off in offsets], axis=1
    )


def wrap_edges(ref, lon):
    ref[0:EDGE] = ref[lon : lon + EDGE]
    ref[lon + EDGE : lon + 2 * EDGE] = ref[EDGE : 2 * EDGE]


def forward_kernel(dims, flags, own, top, bot, w_inner, w_head, hidden_out, slope_out, field_out, xs, hs, fs):
    rows, lon, lon_pad, ch, qp, pieces, piece = dims
    tile = tile_of(lon, 16, 480)
    half = math.sqrt(2.0 / math.pi)
    for j in range(rows + 4):
        if j < 2:
            row = top[0, j]
        elif j < rows + 2:
            row = own[0, j - 2]
        else:
            row = bot[0, j - rows - 2]
        xs[EDGE : EDGE + lon, j * ch : (j + 1) * ch] = row.astype(F32)
    wrap_edges(xs, lon)
    top_ok = flags[0].astype(F32)
    bot_ok = flags[1].astype(F32)

    def inner_step(t, carry):
        start = pl.multiple_of(t * tile, tile)
        for p in range((rows + 2) // 2):
            patch = shifted(xs, start, tile, 2 * p * ch, 4 * ch)
            pre = jnp.dot(patch, w_inner[...], preferred_element_type=F32)
            square = pre * pre
            tanh = jnp.tanh(half * (pre * (1.0 + 0.044715 * square)))
            upper = 0.5 + 0.5 * tanh
            hidden = pre * upper
            slope = upper + (0.5 * half) * pre * (1.0 - tanh * tanh) * (1.0 + (3 * 0.044715) * square)
            for k in range(2):
                i = 2 * p + k
                h = hidden[:, k * ch : (k + 1) * ch]
                s = slope[:, k * ch : (k + 1) * ch]
                if i == 0:
                    h, s = h * top_ok, s * top_ok
                if i == rows + 1:
                    h, s = h * bot_ok, s * bot_ok
                hs[pl.ds(start + EDGE, tile), i * ch : (i + 1) * ch] = h
                slope_out[0, i, pl.ds(start, tile), :] = s.astype(BF16)
                if 1 <= i <= rows:
                    hidden_out[0, i - 1, pl.ds(start, tile), :] = h.astype(BF16)
        return carry

    lax.fori_loop(0, lon // tile, inner_step, 0)
    wrap_edges(hs, lon)
    zero = jnp.zeros((lon_pad - lon, ch), BF16)
    for i in range(rows + 2):
        slope_out[0, i, lon:lon_pad, :] = zero
    for i in range(rows):
        hidden_out[0, i, lon:lon_pad, :] = zero

    def head_step(t, carry):
        start = pl.multiple_of(t * tile, tile)
        for g in range(rows // 2):
            patch = shifted(hs, start, tile, 2 * g * ch, 4 * ch)
            fs[g, pl.ds(start, tile), :] = jnp.dot(patch, w_head[...], preferred_element_type=F32)
        return carry

    lax.fori_loop(0, lon // tile, head_step, 0)
    pair = qp // (rows // 2)
    for g in range(rows // 2):
        fs[g, lon:lon_pad, :] = jnp.zeros((lon_pad - lon, fs.shape[2]), F32)
        fs[g, lon : lon + EDGE, :] = fs[g, 0:EDGE, :]
        fs[g, lon_pad - EDGE : lon_pad, :] = fs[g, lon - EDGE : lon, :]
        for j in range(pieces):
            turned = fs[g, j * piece : (j + 1) * piece, :].T
            field_out[j, 0, g * pair : (g + 1) * pair, :] = turned[:pair].astype(BF16)


def pair_kernel(dims, fields, truth, rate, scale, out, vals, accs):
    members, per, sub, piece = dims
    norm = 2.0 / (members - 1)

    for m in range(members):
        vals[m] = fields[m // per, m % per].astype(F32)
    blocks = piece // LANES

    def step(t, carry):
        r = pl.ds(pl.multiple_of((t // blocks) * 8, 8), 8)
        c = pl.ds(pl.multiple_of((t % blocks) * LANES, LANES), LANES)
        neg = rate[r, :]
        x = [vals[m, r, c] for m in range(members)]
        sums = [None] * members
        for i in range(members):
            for j in range(i + 1, members):
                d = x[j] - x[i]
                w = jnp.exp2(d * d * neg) * d
                sums[i] = w if sums[i] is None else sums[i] + w
                sums[j] = -w if sums[j] is None else sums[j] - w
        y = truth[r, c]
        sc = scale[r, :]
        for i in range(members):
            off = x[i] - y
            near = jnp.exp2(off * off * neg) * off
            accs[i, r, c] = sc * (norm * sums[i] + 2.0 * near)
        return carry

    lax.fori_loop(0, (sub // 8) * blocks, step, 0)
    for m in range(members):
        out[m // per, m % per] = accs[m].astype(BF16)


def backward_kernel(dims, own, top, bot, hidden, slope, feats, w_back, w_grad, grad_out, sums_out, gs, ss, acc_in, acc_hd):
    rows, lon, lon_pad, ch, vp, pieces, piece, low, span = dims
    ext = (rows + 4) * vp
    step_m = pl.program_id(0)

    @pl.when(step_m == 0)
    def _():
        acc_in[...] = jnp.zeros_like(acc_in)
        acc_hd[...] = jnp.zeros_like(acc_hd)

    for j in range(pieces):
        cols = slice(j * piece, (j + 1) * piece)
        gs[1, 0 : 2 * vp, cols] = top[j, 0]
        gs[1, 2 * vp : ext - 2 * vp, cols] = own[j, 0]
        gs[1, ext - 2 * vp : ext, cols] = bot[j, 0]

    def roll_step(t, carry):
        r = pl.ds(pl.multiple_of(t * 16, 16), 16)
        block = gs[1, r, :].astype(F32)
        gs[0, r, :] = pltpu.roll(block, lon_pad - 1, 1).astype(BF16)
        gs[2, r, :] = pltpu.roll(block, 1, 1).astype(BF16)
        return carry

    lax.fori_loop(0, ext // 16, roll_step, 0)
    tile = tile_of(lon_pad, LANES, 512)

    def hidden_step(t, carry):
        start = pl.multiple_of(t * tile, tile)
        for p in range((rows + 2) // 2):
            patch = jnp.concatenate(
                [gs[b, 2 * p * vp : (2 * p + 4) * vp, pl.ds(start, tile)] for b in range(3)], axis=0
            )
            back = lax.dot_general(
                patch, w_back[...], (((0,), (0,)), ((), ())), preferred_element_type=F32
            )
            for k in range(2):
                i = 2 * p + k
                ss[pl.ds(start + EDGE, tile), i * ch : (i + 1) * ch] = back[
                    :, k * ch : (k + 1) * ch
                ] * slope[0, i, pl.ds(start, tile), :].astype(F32)
        for g in range(rows // 2):
            base = 2 * g * vp + low
            patch = jnp.concatenate(
                [gs[b, base : base + span, pl.ds(start, tile)] for b in range(3)], axis=0
            )
            act = jnp.concatenate(
                [hidden[0, 2 * g + k, pl.ds(start, tile), :] for k in range(2)], axis=1
            )
            acc_hd[...] += jnp.dot(patch, act, preferred_element_type=F32)
        return carry

    lax.fori_loop(0, lon_pad // tile, hidden_step, 0)
    wrap_edges(ss, lon)
    tile2 = tile_of(lon, 16, 480)

    def feature_step(t, carry):
        start = pl.multiple_of(t * tile2, tile2)
        for g in range(rows // 2):
            patch = shifted(ss, start, tile2, 2 * g * ch, 4 * ch, (1, 0, -1))
            grad = jnp.dot(patch, w_grad[...], preferred_element_type=F32)
            for k in range(2):
                grad_out[0, 2 * g + k, pl.ds(start, tile2), :] = grad[
                    :, k * ch : (k + 1) * ch
                ].astype(BF16)
            act = jnp.concatenate(
                [feats[0, 2 * g + k, pl.ds(start, tile2), :] for k in range(2)], axis=1
            )
            acc_in[...] += lax.dot_general(
                act, patch, (((0,), (0,)), ((), ())), preferred_element_type=F32
            )
        return carry

    lax.fori_loop(0, lon // tile2, feature_step, 0)

    @pl.when(step_m == pl.num_programs(0) - 1)
    def _():
        for a in range(3):
            for b in range(3):
                inner = None
                head = None
                for k in range(2):
                    n = k + 2 - a
                    part = acc_in[k * ch : (k + 1) * ch, (b * 4 + n) * ch : (b * 4 + n + 1) * ch]
                    inner = part if inner is None else inner + part
                    n = k + 3 - a
                    at = b * span + n * vp - low
                    part = acc_hd[at : at + vp, k * ch : (k + 1) * ch]
                    head = part if head is None else head + part
                q = 3 * a + b
                sums_out[q * ch : (q + 1) * ch, :] = inner
                at = 9 * ch + q * vp
                sums_out[at : at + vp, :] = head


def forward_weights(kernel, width):
    ch, outs = kernel.shape[2], kernel.shape[3]
    kernel = jnp.pad(kernel, ((0, 0), (0, 0), (0, 0), (0, width - outs)))
    cols = []
    for out_row in range(2):
        taps = jnp.pad(kernel, ((out_row, 1 - out_row), (0, 0), (0, 0), (0, 0)))
        cols.append(jnp.moveaxis(taps, 0, 1))
    return jnp.stack(cols, axis=3).reshape(3 * 4 * ch, 2 * width)


def backward_weights(kernel, width):
    ch, outs = kernel.shape[2], kernel.shape[3]
    kernel = jnp.pad(kernel, ((0, 0), (0, 0), (0, 0), (0, width - outs)))[::-1]
    cols = []
    for out_row in range(2):
        taps = jnp.pad(kernel, ((out_row, 1 - out_row), (0, 0), (0, 0), (0, 0)))
        cols.append(jnp.transpose(taps, (1, 0, 3, 2)))
    return jnp.stack(cols, axis=3).reshape(3 * 4 * width, 2 * ch)


def neighbours(tail, head, axis):
    count = lax.axis_size(axis)
    before = lax.ppermute(tail, axis, [(i, i + 1) for i in range(count - 1)])
    after = lax.ppermute(head, axis, [(i + 1, i) for i in range(count - 1)])
    return before, after


def reduce_all(values, axes):
    count = math.prod(lax.axis_size(a) for a in axes)
    rows, width = values.shape
    part = -(-rows // (16 * count)) * 16
    padded = jnp.pad(values, ((0, part * count - rows), (0, 0))).astype(BF16)
    got = lax.all_to_all(padded, axes, 0, 0, tiled=True)
    summed = jnp.sum(got.reshape(count, part, width).astype(F32), axis=0).astype(BF16)
    spread = jnp.broadcast_to(summed[None], (count, part, width))
    full = lax.all_to_all(spread, axes, 0, 0)
    return full.reshape(count * part, width)[:rows].astype(F32)


def shards(features, conv_inner, conv_head, truth, kernel_width, var_weight):
    per, rows, lon, ch = features.shape
    variables = conv_head.shape[3]
    pieces = lax.axis_size("mem")
    members = per * pieces
    vp = -(-variables // 8) * 8
    qp = rows * vp
    piece = -(-lon // (LANES * pieces)) * LANES
    if lon + 2 * EDGE > piece * pieces:
        piece += LANES
    lon_pad = piece * pieces
    assert rows % 2 == 0 and lon % 16 == 0 and (2 * vp) % 16 == 0 and 2 * vp <= 256
    low = vp // 16 * 16
    span = -(-(5 * vp - low) // 16) * 16

    top, bot = neighbours(features[:, rows - 2 :], features[:, :2], "lat")
    at = lax.axis_index("lat")
    flags = jnp.stack([at > 0, at < lax.axis_size("lat") - 1]).astype(jnp.int32)

    w_inner = forward_weights(conv_inner, ch)
    w_head = jnp.pad(forward_weights(conv_head, vp), ((0, 0), (0, 256 - 2 * vp)))
    w_back = backward_weights(conv_head, vp)
    w_grad = backward_weights(conv_inner, ch)

    params = functools.partial(pltpu.CompilerParams, vmem_limit_bytes=VMEM_LIMIT)
    whole = lambda shape: pl.BlockSpec(shape, lambda m: (0,) * len(shape))
    member = lambda shape: pl.BlockSpec((1,) + shape, lambda m: (m,) + (0,) * len(shape))
    spread = lambda n: pl.BlockSpec((pieces, 1, n, piece), lambda m: (0, m, 0, 0))

    macs = 2 * lon * 12 * ch * 2 * ch * per
    hidden, slope, field = pl.pallas_call(
        functools.partial(forward_kernel, (rows, lon, lon_pad, ch, qp, pieces, piece)),
        grid=(per,),
        in_specs=[
            pl.BlockSpec(memory_space=pltpu.SMEM),
            member((rows, lon, ch)),
            member((2, lon, ch)),
            member((2, lon, ch)),
            whole(w_inner.shape),
            whole(w_head.shape),
        ],
        out_specs=[member((rows, lon_pad, ch)), member((rows + 2, lon_pad, ch)), spread(qp)],
        out_shape=[
            jax.ShapeDtypeStruct((per, rows, lon_pad, ch), BF16),
            jax.ShapeDtypeStruct((per, rows + 2, lon_pad, ch), BF16),
            jax.ShapeDtypeStruct((pieces, per, qp, piece), BF16),
        ],
        scratch_shapes=[
            pltpu.VMEM((lon + 2 * EDGE, (rows + 4) * ch), F32),
            pltpu.VMEM((lon + 2 * EDGE, (rows + 2) * ch), F32),
            pltpu.VMEM((rows // 2, lon_pad, 256), F32),
        ],
        compiler_params=params(),
        cost_estimate=pl.CostEstimate(flops=3 * macs, bytes_accessed=24 << 20, transcendentals=0),
        name="forward",
    )(flags, features, top, bot, w_inner, w_head)

    traded = lax.all_to_all(field, "mem", 0, 0, tiled=True)

    truth_rows = jnp.moveaxis(truth, 1, 0)
    truth_rows = jnp.pad(truth_rows, ((0, 0), (0, vp - variables), (0, 0))).reshape(qp, lon)
    middle = jnp.zeros((qp, lon_pad - lon - 2 * EDGE), F32)
    truth_rows = jnp.concatenate(
        [truth_rows, truth_rows[:, :EDGE], middle, truth_rows[:, lon - EDGE :]], axis=1
    )
    truth_piece = lax.dynamic_slice_in_dim(truth_rows, lax.axis_index("mem") * piece, piece, 1)
    inverse = 1.0 / (kernel_width * kernel_width)
    spread_param = lambda v: jnp.broadcast_to(
        jnp.tile(jnp.pad(v, (0, vp - variables)), rows)[:, None], (qp, LANES)
    )
    rate = spread_param((-0.5 * math.log2(math.e)) * inverse)
    scale = spread_param(var_weight * inverse)
    sub = 16
    row_block = lambda width: pl.BlockSpec((sub, width), lambda i: (i, 0))
    field_block = pl.BlockSpec((pieces, per, sub, piece), lambda i: (0, 0, i, 0))
    gradient = pl.pallas_call(
        functools.partial(pair_kernel, (members, per, sub, piece)),
        grid=(qp // sub,),
        in_specs=[field_block, row_block(piece), row_block(LANES), row_block(LANES)],
        out_specs=field_block,
        out_shape=jax.ShapeDtypeStruct(traded.shape, BF16),
        scratch_shapes=[pltpu.VMEM((members, sub, piece), F32)] * 2,
        compiler_params=params(),
        cost_estimate=pl.CostEstimate(
            flops=4 * members * members * qp * piece,
            bytes_accessed=4 * members * qp * piece,
            transcendentals=members * members // 2 * qp * piece,
        ),
        name="pairs",
    )(traded, truth_piece, rate, scale)

    own = lax.all_to_all(gradient, "mem", 0, 0, tiled=True)
    g_top, g_bot = neighbours(own[:, :, qp - 2 * vp :], own[:, :, : 2 * vp], "lat")
    sums_rows = 9 * (ch + vp)
    grad_features, sums = pl.pallas_call(
        functools.partial(backward_kernel, (rows, lon, lon_pad, ch, vp, pieces, piece, low, span)),
        grid=(per,),
        in_specs=[
            spread(qp),
            spread(2 * vp),
            spread(2 * vp),
            member((rows, lon_pad, ch)),
            member((rows + 2, lon_pad, ch)),
            member((rows, lon, ch)),
            whole(w_back.shape),
            whole(w_grad.shape),
        ],
        out_specs=[member((rows, lon, ch)), whole((sums_rows, ch))],
        out_shape=[
            jax.ShapeDtypeStruct(features.shape, BF16),
            jax.ShapeDtypeStruct((sums_rows, ch), F32),
        ],
        scratch_shapes=[
            pltpu.VMEM((3, (rows + 4) * vp, lon_pad), BF16),
            pltpu.VMEM((lon_pad + 2 * EDGE, (rows + 2) * ch), F32),
            pltpu.VMEM((2 * ch, 12 * ch), F32),
            pltpu.VMEM((3 * span, 2 * ch), F32),
        ],
        compiler_params=params(),
        cost_estimate=pl.CostEstimate(flops=5 * macs, bytes_accessed=24 << 20, transcendentals=0),
        name="backward",
    )(own, g_top, g_bot, hidden, slope, features, w_back, w_grad)

    total = reduce_all(sums, ("mem", "lat"))
    points = rows * lax.axis_size("lat") * lon
    inner_sum = total[: 9 * ch].reshape(3, 3, ch, ch)
    head_sum = total[9 * ch :].reshape(3, 3, vp, ch)[:, :, :variables]
    return (grad_features, inner_sum / points, jnp.swapaxes(head_sum, 2, 3) / points)


def solution(mesh):
    in_specs = (P("mem", "lat", None, None), P(), P(), P(None, "lat", None), P(), P())
    out_specs = (P("mem", "lat", None, None), P(), P())
    return jax.shard_map(shards, mesh=mesh, in_specs=in_specs, out_specs=out_specs, check_vma=False)
```

```python
import functools
import math

import jax
import jax.numpy as jnp
from jax import lax
from jax.experimental import pallas as pl
from jax.experimental.pallas import tpu as pltpu
from jax.sharding import PartitionSpec as P


BF16 = jnp.bfloat16
F32 = jnp.float32
LANES = 128
EDGE = 16
VMEM_LIMIT = 60 * 1024 * 1024
TILE = 480
AHEAD = 2
BACK = 2


def tile_of(count, step, most):
    return max(t for t in range(step, most + 1, step) if count % t == 0)


def wrap_edges(ref, lon):
    ref[0:EDGE] = ref[lon : lon + EDGE]
    ref[lon + EDGE : lon + 2 * EDGE] = ref[EDGE : 2 * EDGE]


def moved(values, offset, tile):
    if offset:
        values = pltpu.roll(values, (-offset) % values.shape[0], 0)
    return values[EDGE : EDGE + tile]


def three_taps(window, weights, offsets, tile):
    total = None
    for b, offset in enumerate(offsets):
        part = jnp.dot(window, weights[b], preferred_element_type=F32)
        part = moved(part, offset, tile)
        total = part if total is None else total + part
    return total


def forward_kernel(dims, flags, own, top, bot, w_inner, w_head, *refs):
    rows, lon, lon_pad, ch, qp, pieces, piece = dims
    hidden_out, slope_out, field_out, xs, hs, fs = refs[-6:]
    tile = tile_of(lon, 16, TILE)
    half = math.sqrt(2.0 / math.pi)
    for j in range(rows + 4):
        if j < 2:
            row = top[0, j]
        elif j < rows + 2:
            row = own[0, j - 2]
        else:
            row = bot[0, j - rows - 2]
        xs[EDGE : EDGE + lon, j * ch : (j + 1) * ch] = row
    wrap_edges(xs, lon)
    top_ok = flags[0].astype(F32)
    bot_ok = flags[1].astype(F32)

    def inner_step(t, carry):
        start = pl.multiple_of(t * tile, tile)
        for p in range((rows + 2) // 2):
            window = xs[pl.ds(start, tile + 2 * EDGE), 2 * p * ch : (2 * p + 4) * ch]
            pre = three_taps(window, w_inner, (-1, 0, 1), tile)
            square = pre * pre
            tanh = jnp.tanh(pre * (half + (half * 0.044715) * square))
            upper = 0.5 + 0.5 * tanh
            hidden = pre * upper
            slope = upper + hidden * (1.0 - upper) * (2.0 * half + (6.0 * half * 0.044715) * square)
            for k in range(2):
                i = 2 * p + k
                h = hidden[:, k * ch : (k + 1) * ch]
                s = slope[:, k * ch : (k + 1) * ch]
                if i == 0:
                    h, s = h * top_ok, s * top_ok
                if i == rows + 1:
                    h, s = h * bot_ok, s * bot_ok
                h = h.astype(BF16)
                hs[pl.ds(start + EDGE, tile), i * ch : (i + 1) * ch] = h
                slope_out[0, i, pl.ds(start, tile), :] = s.astype(BF16)
                if 1 <= i <= rows:
                    hidden_out[0, i - 1, pl.ds(start, tile), :] = h
        return carry

    lax.fori_loop(0, lon // tile, inner_step, 0)
    wrap_edges(hs, lon)
    zero = jnp.zeros((lon_pad - lon, ch), BF16)
    for i in range(rows + 2):
        slope_out[0, i, lon:lon_pad, :] = zero
    for i in range(rows):
        hidden_out[0, i, lon:lon_pad, :] = zero

    def head_step(t, carry):
        start = pl.multiple_of(t * tile, tile)
        for g in range(rows // 2):
            window = hs[pl.ds(start, tile + 2 * EDGE), 2 * g * ch : (2 * g + 4) * ch]
            fs[g, pl.ds(start, tile), :] = three_taps(window, w_head, (-1, 0, 1), tile)
        return carry

    lax.fori_loop(0, lon // tile, head_step, 0)
    pair = qp // (rows // 2)
    for g in range(rows // 2):
        fs[g, lon:lon_pad, :] = jnp.zeros((lon_pad - lon, fs.shape[2]), F32)
        fs[g, lon : lon + EDGE, :] = fs[g, 0:EDGE, :]
        fs[g, lon_pad - EDGE : lon_pad, :] = fs[g, lon - EDGE : lon, :]
        for j in range(pieces):
            turned = fs[g, j * piece : (j + 1) * piece, :].T
            field_out[j, 0, g * pair : (g + 1) * pair, :] = turned[:pair].astype(BF16)


def pair_kernel(dims, truth, rate, scale, *refs):
    members, taken, given, sub, piece = dims
    fields, outs, vals, accs = refs[:taken], refs[taken : taken + given], refs[-2], refs[-1]
    norm = 2.0 / (members - 1)
    pieces = fields[0].shape[0]
    for j in range(pieces):
        m = j * (members // pieces)
        for ref in fields:
            for k in range(ref.shape[1]):
                vals[m] = ref[j, k].astype(F32)
                m += 1
    blocks = piece // LANES

    def step(t, carry):
        r = pl.ds(pl.multiple_of((t // blocks) * 8, 8), 8)
        c = pl.ds(pl.multiple_of((t % blocks) * LANES, LANES), LANES)
        neg = rate[r, :]
        x = [vals[m, r, c] for m in range(members)]
        sums = [None] * members
        for i in range(members):
            for j in range(i + 1, members):
                d = x[j] - x[i]
                w = jnp.exp2(d * d * neg) * d
                sums[i] = w if sums[i] is None else sums[i] + w
                sums[j] = -w if sums[j] is None else sums[j] - w
        y = truth[r, c]
        sc = scale[r, :]
        for i in range(members):
            off = x[i] - y
            near = jnp.exp2(off * off * neg) * off
            accs[i, r, c] = sc * (norm * sums[i] + 2.0 * near)
        return carry

    lax.fori_loop(0, (sub // 8) * blocks, step, 0)
    for j in range(pieces):
        m = j * (members // pieces)
        for ref in outs:
            for k in range(ref.shape[1]):
                ref[j, k] = accs[m].astype(BF16)
                m += 1


def backward_kernel(dims, own, top, bot, hidden, slope, feats, w_back, *refs):
    rows, lon, lon_pad, ch, vp, pieces, piece, low, span = dims
    back_out, sums_out, gs, fx, acc_in, acc_hd = refs[-6:]
    ext = (rows + 4) * vp
    step_m = pl.program_id(0)

    @pl.when(step_m == 0)
    def _():
        acc_in[...] = jnp.zeros_like(acc_in)
        acc_hd[...] = jnp.zeros_like(acc_hd)

    for j in range(pieces):
        cols = slice(j * piece, (j + 1) * piece)
        gs[1, 0 : 2 * vp, cols] = top[j, 0]
        gs[1, 2 * vp : ext - 2 * vp, cols] = own[j, 0]
        gs[1, ext - 2 * vp : ext, cols] = bot[j, 0]
    for t in range(ext // 16):
        r = slice(t * 16, (t + 1) * 16)
        block = gs[1, r, :].astype(F32)
        gs[0, r, :] = pltpu.roll(block, lon_pad - 1, 1).astype(BF16)
        gs[2, r, :] = pltpu.roll(block, 1, 1).astype(BF16)
    for r in range(rows):
        fx[EDGE : EDGE + lon, r * ch : (r + 1) * ch] = feats[0, r]
    wrap_edges(fx, lon)
    fx[lon + 2 * EDGE :] = jnp.zeros((lon_pad - lon, rows * ch), BF16)
    tile = tile_of(lon_pad, LANES, 512)

    def step(t, carry):
        start = pl.multiple_of(t * tile, tile)
        rows_back = []
        for p in range((rows + 2) // 2):
            patch = jnp.concatenate(
                [gs[b, 2 * p * vp : (2 * p + 4) * vp, pl.ds(start, tile)] for b in range(3)], axis=0
            )
            back = lax.dot_general(
                patch, w_back[...], (((0,), (0,)), ((), ())), preferred_element_type=F32
            )
            for k in range(2):
                i = 2 * p + k
                part = back[:, k * ch : (k + 1) * ch] * slope[0, i, pl.ds(start, tile), :].astype(F32)
                part = part.astype(BF16)
                back_out[0, i, pl.ds(start, tile), :] = part
                rows_back.append(part)
        for g in range(rows // 2):
            base = 2 * g * vp + low
            patch = jnp.concatenate(
                [gs[b, base : base + span, pl.ds(start, tile)] for b in range(3)], axis=0
            )
            act = jnp.concatenate(
                [hidden[0, 2 * g + k, pl.ds(start, tile), :] for k in range(2)], axis=1
            )
            acc_hd[...] += jnp.dot(patch, act, preferred_element_type=F32)
            window = fx[pl.ds(start, tile + 2 * EDGE), 2 * g * ch : (2 * g + 2) * ch].astype(F32)
            act = jnp.concatenate(
                [moved(window, off, tile).astype(BF16) for off in (-1, 0, 1)], axis=1
            )
            back = jnp.concatenate(rows_back[2 * g : 2 * g + 4], axis=1)
            acc_in[...] += lax.dot_general(
                act, back, (((0,), (0,)), ((), ())), preferred_element_type=F32
            )
        return carry

    lax.fori_loop(0, lon_pad // tile, step, 0)

    @pl.when(step_m == pl.num_programs(0) - 1)
    def _():
        for a in range(3):
            for b in range(3):
                inner = None
                head = None
                for k in range(2):
                    n = k + 2 - a
                    at = b * 2 * ch + k * ch
                    part = acc_in[at : at + ch, n * ch : (n + 1) * ch]
                    inner = part if inner is None else inner + part
                    n = k + 3 - a
                    at = b * span + n * vp - low
                    part = acc_hd[at : at + vp, k * ch : (k + 1) * ch]
                    head = part if head is None else head + part
                q = 3 * a + b
                sums_out[q * ch : (q + 1) * ch, :] = inner
                at = 9 * ch + q * vp
                sums_out[at : at + vp, :] = head


def feature_kernel(dims, back, w_grad, grad_out, bs):
    rows, lon, ch = dims
    for i in range(rows + 2):
        bs[EDGE : EDGE + lon, i * ch : (i + 1) * ch] = back[0, i, :lon]
    wrap_edges(bs, lon)
    tile = tile_of(lon, 16, TILE)

    def step(t, carry):
        start = pl.multiple_of(t * tile, tile)
        for g in range(rows // 2):
            window = bs[pl.ds(start, tile + 2 * EDGE), 2 * g * ch : (2 * g + 4) * ch]
            grad = three_taps(window, w_grad, (1, 0, -1), tile)
            for k in range(2):
                grad_out[0, 2 * g + k, pl.ds(start, tile), :] = grad[
                    :, k * ch : (k + 1) * ch
                ].astype(BF16)
        return carry

    lax.fori_loop(0, lon // tile, step, 0)


def forward_weights(kernel, width):
    ch, outs = kernel.shape[2], kernel.shape[3]
    kernel = jnp.pad(kernel, ((0, 0), (0, 0), (0, 0), (0, width - outs)))
    cols = []
    for out_row in range(2):
        taps = jnp.pad(kernel, ((out_row, 1 - out_row), (0, 0), (0, 0), (0, 0)))
        cols.append(jnp.moveaxis(taps, 0, 1))
    return jnp.stack(cols, axis=3).reshape(3, 4 * ch, 2 * width)


def backward_weights(kernel, width):
    ch, outs = kernel.shape[2], kernel.shape[3]
    kernel = jnp.pad(kernel, ((0, 0), (0, 0), (0, 0), (0, width - outs)))[::-1]
    cols = []
    for out_row in range(2):
        taps = jnp.pad(kernel, ((out_row, 1 - out_row), (0, 0), (0, 0), (0, 0)))
        cols.append(jnp.transpose(taps, (1, 0, 3, 2)))
    return jnp.stack(cols, axis=3).reshape(3, 4 * width, 2 * ch)


def groups_of(count, groups):
    out, first = [], 0
    for g in range(min(groups, count)):
        size = -(-(count - first) // (min(groups, count) - g))
        out.append((first, size))
        first += size
    return out


def neighbours(tail, head, axis):
    count = lax.axis_size(axis)
    before = lax.ppermute(tail, axis, [(i, i + 1) for i in range(count - 1)])
    after = lax.ppermute(head, axis, [(i + 1, i) for i in range(count - 1)])
    return before, after


def reduce_all(values, axes):
    count = math.prod(lax.axis_size(a) for a in axes)
    rows, width = values.shape
    part = -(-rows // (16 * count)) * 16
    padded = jnp.pad(values, ((0, part * count - rows), (0, 0))).astype(BF16)
    got = lax.all_to_all(padded, axes, 0, 0, tiled=True)
    summed = jnp.sum(got.reshape(count, part, width).astype(F32), axis=0).astype(BF16)
    spread = jnp.broadcast_to(summed[None], (count, part, width))
    full = lax.all_to_all(spread, axes, 0, 0)
    return full.reshape(count * part, width)[:rows].astype(F32)


def shards(features, conv_inner, conv_head, truth, kernel_width, var_weight):
    per, rows, lon, ch = features.shape
    variables = conv_head.shape[3]
    pieces = lax.axis_size("mem")
    members = per * pieces
    vp = -(-variables // 8) * 8
    qp = rows * vp
    piece = -(-lon // (LANES * pieces)) * LANES
    while lon + 2 * EDGE > piece * pieces:
        piece += LANES
    lon_pad = piece * pieces
    assert rows % 2 == 0 and lon % 16 == 0 and (2 * vp) % 16 == 0 and 2 * vp <= 256
    low = vp // 16 * 16
    span = -(-(5 * vp - low) // 16) * 16

    at = lax.axis_index("lat")
    flags = jnp.stack([at > 0, at < lax.axis_size("lat") - 1]).astype(jnp.int32)

    w_inner = forward_weights(conv_inner, ch)
    w_head = jnp.pad(forward_weights(conv_head, vp), ((0, 0), (0, 0), (0, 256 - 2 * vp)))
    w_back = backward_weights(conv_head, vp).reshape(12 * vp, 2 * ch)
    w_grad = backward_weights(conv_inner, ch)

    params = functools.partial(pltpu.CompilerParams, vmem_limit_bytes=VMEM_LIMIT)
    whole = lambda shape: pl.BlockSpec(shape, lambda m: (0,) * len(shape))
    member = lambda shape, base=0: pl.BlockSpec((1,) + shape, lambda m: (base + m,) + (0,) * len(shape))
    spread = lambda n: pl.BlockSpec((pieces, 1, n, piece), lambda m: (0, m, 0, 0))
    macs = 2 * lon * 12 * ch * 2 * ch

    kept_shapes = [
        jax.ShapeDtypeStruct((per, rows, lon_pad, ch), BF16),
        jax.ShapeDtypeStruct((per, rows + 2, lon_pad, ch), BF16),
    ]
    ahead, behind = groups_of(per, AHEAD), groups_of(per, BACK)

    def forward(first, count, kept):
        mine = features[first : first + count]
        top, bot = neighbours(mine[:, rows - 2 :], mine[:, :2], "lat")
        return pl.pallas_call(
            functools.partial(forward_kernel, (rows, lon, lon_pad, ch, qp, pieces, piece)),
            grid=(count,),
            in_specs=[
                pl.BlockSpec(memory_space=pltpu.SMEM),
                member((rows, lon, ch), first),
                member((2, lon, ch)),
                member((2, lon, ch)),
                whole(w_inner.shape),
                whole(w_head.shape),
            ]
            + [pl.BlockSpec(memory_space=pl.ANY)] * len(kept),
            out_specs=[
                member((rows, lon_pad, ch), first),
                member((rows + 2, lon_pad, ch), first),
                spread(qp),
            ],
            out_shape=kept_shapes + [jax.ShapeDtypeStruct((pieces, count, qp, piece), BF16)],
            input_output_aliases={6 + k: k for k in range(len(kept))},
            scratch_shapes=[
                pltpu.VMEM((lon + 2 * EDGE, (rows + 4) * ch), BF16),
                pltpu.VMEM((lon + 2 * EDGE, (rows + 2) * ch), BF16),
                pltpu.VMEM((rows // 2, lon_pad, 256), F32),
            ],
            compiler_params=params(),
            cost_estimate=pl.CostEstimate(
                flops=3 * macs * count, bytes_accessed=(6 << 20) * count, transcendentals=0
            ),
            name="forward",
        )(flags, features, top, bot, w_inner, w_head, *kept)

    kept, traded = [], []
    for first, count in ahead:
        *kept, field = forward(first, count, kept)
        traded.append(lax.all_to_all(field, "mem", 0, 0, tiled=True))

    truth_rows = jnp.moveaxis(truth, 1, 0)
    truth_rows = jnp.pad(truth_rows, ((0, 0), (0, vp - variables), (0, 0))).reshape(qp, lon)
    middle = jnp.zeros((qp, lon_pad - lon - 2 * EDGE), F32)
    truth_rows = jnp.concatenate(
        [truth_rows, truth_rows[:, :EDGE], middle, truth_rows[:, lon - EDGE :]], axis=1
    )
    truth_piece = lax.dynamic_slice_in_dim(truth_rows, lax.axis_index("mem") * piece, piece, 1)
    inverse = 1.0 / (kernel_width * kernel_width)
    spread_param = lambda v: jnp.broadcast_to(
        jnp.tile(jnp.pad(v, (0, vp - variables)), rows)[:, None], (qp, LANES)
    )
    rate = spread_param((-0.5 * math.log2(math.e)) * inverse)
    scale = spread_param(var_weight * inverse)
    sub = 16
    row_block = lambda width: pl.BlockSpec((sub, width), lambda i: (i, 0))
    field_block = lambda count: pl.BlockSpec((pieces, count, sub, piece), lambda i: (0, 0, i, 0))
    gradient = pl.pallas_call(
        functools.partial(pair_kernel, (members, len(ahead), len(behind), sub, piece)),
        grid=(qp // sub,),
        in_specs=[row_block(piece), row_block(LANES), row_block(LANES)]
        + [field_block(count) for _, count in ahead],
        out_specs=[field_block(count) for _, count in behind],
        out_shape=[
            jax.ShapeDtypeStruct((pieces, count, qp, piece), BF16) for _, count in behind
        ],
        scratch_shapes=[pltpu.VMEM((members, sub, piece), F32)] * 2,
        compiler_params=params(),
        cost_estimate=pl.CostEstimate(
            flops=4 * members * members * qp * piece,
            bytes_accessed=4 * members * qp * piece,
            transcendentals=members * members // 2 * qp * piece,
        ),
        name="pairs",
    )(truth_piece, rate, scale, *traded)

    sums_rows = 9 * (ch + vp)

    def backward(own, first, count, back):
        g_top, g_bot = neighbours(own[:, :, qp - 2 * vp :], own[:, :, : 2 * vp], "lat")
        return pl.pallas_call(
            functools.partial(
                backward_kernel, (rows, lon, lon_pad, ch, vp, pieces, piece, low, span)
            ),
            grid=(count,),
            in_specs=[
                spread(qp),
                spread(2 * vp),
                spread(2 * vp),
                member((rows, lon_pad, ch), first),
                member((rows + 2, lon_pad, ch), first),
                member((rows, lon, ch), first),
                whole(w_back.shape),
            ]
            + [pl.BlockSpec(memory_space=pl.ANY)] * len(back),
            out_specs=[member((rows + 2, lon_pad, ch), first), whole((sums_rows, ch))],
            out_shape=[kept_shapes[1], jax.ShapeDtypeStruct((sums_rows, ch), F32)],
            input_output_aliases={7 + k: k for k in range(len(back))},
            scratch_shapes=[
                pltpu.VMEM((3, (rows + 4) * vp, lon_pad), BF16),
                pltpu.VMEM((lon_pad + 2 * EDGE, rows * ch), BF16),
                pltpu.VMEM((6 * ch, 4 * ch), F32),
                pltpu.VMEM((3 * span, 2 * ch), F32),
            ],
            compiler_params=params(),
            cost_estimate=pl.CostEstimate(
                flops=4 * macs * count, bytes_accessed=(6 << 20) * count, transcendentals=0
            ),
            name="backward",
        )(own, g_top, g_bot, *kept, features, w_back, *back)

    owned, back, sums = [], [], None
    for g in gradient:
        owned.append(lax.all_to_all(g, "mem", 0, 0, tiled=True))
    for own, chunk in zip(owned, behind):
        *back, part = backward(own, *chunk, back)
        sums = part if sums is None else sums + part
    grad_features = pl.pallas_call(
        functools.partial(feature_kernel, (rows, lon, ch)),
        grid=(per,),
        in_specs=[member((rows + 2, lon_pad, ch)), whole(w_grad.shape)],
        out_specs=member((rows, lon, ch)),
        out_shape=jax.ShapeDtypeStruct(features.shape, BF16),
        scratch_shapes=[pltpu.VMEM((lon + 2 * EDGE, (rows + 2) * ch), BF16)],
        compiler_params=params(),
        cost_estimate=pl.CostEstimate(
            flops=macs * per, bytes_accessed=(4 << 20) * per, transcendentals=0
        ),
        name="features",
    )(*back, w_grad)

    total = reduce_all(sums, ("mem", "lat"))
    points = rows * lax.axis_size("lat") * lon
    inner_sum = total[: 9 * ch].reshape(3, 3, ch, ch)
    head_sum = total[9 * ch :].reshape(3, 3, vp, ch)[:, :, :variables]
    return (grad_features, inner_sum / points, jnp.swapaxes(head_sum, 2, 3) / points)


def solution(mesh):
    in_specs = (P("mem", "lat", None, None), P(), P(), P(None, "lat", None), P(), P())
    out_specs = (P("mem", "lat", None, None), P(), P())

    return jax.shard_map(shards, mesh=mesh, in_specs=in_specs, out_specs=out_specs, check_vma=False)
```

```python
import functools
import math

import jax
import jax.numpy as jnp
from jax import lax
from jax.experimental import pallas as pl
from jax.experimental.pallas import tpu as pltpu
from jax.sharding import PartitionSpec as P


BF16 = jnp.bfloat16
F32 = jnp.float32
LANES = 128
EDGE = 16
MIB = 1024 * 1024
FWD_MIB, PAIR_MIB, BACK_MIB, LAST_MIB = 60, 44, 44, 56
TILE = 480
AHEAD = (2, 1)
BEHIND = 2


def tile_of(count, step, most):
    return max(t for t in range(step, most + 1, step) if count % t == 0)


def wrap_edges(ref, lon):
    ref[0:EDGE] = ref[lon : lon + EDGE]
    ref[lon + EDGE : lon + 2 * EDGE] = ref[EDGE : 2 * EDGE]


def moved(values, offset, tile):
    if offset:
        values = pltpu.roll(values, (-offset) % values.shape[0], 0)
    return values[EDGE : EDGE + tile]


def three_taps(window, weights, offsets, tile):
    total = None
    for b, offset in enumerate(offsets):
        part = jnp.dot(window, weights[b], preferred_element_type=F32)
        part = moved(part, offset, tile)
        total = part if total is None else total + part
    return total


def forward_kernel(dims, flags, own, top, bot, w_inner, w_head, *refs):
    rows, lon, lon_pad, ch, qp, pieces, piece, relay = dims
    relayed = refs[0] if relay else None
    hidden_out, slope_out, field_out, xs, hs, fs = refs[-6:]
    tile = tile_of(lon, 16, TILE)
    half = math.sqrt(2.0 / math.pi)
    for j in range(rows + 4):
        if j < 2:
            row = top[0, j]
            if relayed is not None:
                row = jnp.where(flags[2] != 0, relayed[0, j], row)
        elif j < rows + 2:
            row = own[0, j - 2]
        else:
            row = bot[0, j - rows - 2]
            if relayed is not None:
                row = jnp.where(flags[3] != 0, relayed[0, j - rows - 2], row)
        xs[EDGE : EDGE + lon, j * ch : (j + 1) * ch] = row
    wrap_edges(xs, lon)
    top_ok = flags[0].astype(F32)
    bot_ok = flags[1].astype(F32)

    def inner_step(t, carry):
        start = pl.multiple_of(t * tile, tile)
        for p in range((rows + 2) // 2):
            window = xs[pl.ds(start, tile + 2 * EDGE), 2 * p * ch : (2 * p + 4) * ch]
            pre = three_taps(window, w_inner, (-1, 0, 1), tile)
            square = pre * pre
            tanh = jnp.tanh(pre * (half + (half * 0.044715) * square))
            upper = 0.5 + 0.5 * tanh
            hidden = pre * upper
            slope = upper + hidden * (1.0 - upper) * (2.0 * half + (6.0 * half * 0.044715) * square)
            for k in range(2):
                i = 2 * p + k
                h = hidden[:, k * ch : (k + 1) * ch]
                s = slope[:, k * ch : (k + 1) * ch]
                if i == 0:
                    h, s = h * top_ok, s * top_ok
                if i == rows + 1:
                    h, s = h * bot_ok, s * bot_ok
                h = h.astype(BF16)
                hs[pl.ds(start + EDGE, tile), i * ch : (i + 1) * ch] = h
                slope_out[0, i, pl.ds(start, tile), :] = s.astype(BF16)
                if 1 <= i <= rows:
                    hidden_out[0, i - 1, pl.ds(start, tile), :] = h
        return carry

    lax.fori_loop(0, lon // tile, inner_step, 0)
    wrap_edges(hs, lon)
    zero = jnp.zeros((lon_pad - lon, ch), BF16)
    for i in range(rows + 2):
        slope_out[0, i, lon:lon_pad, :] = zero
    for i in range(rows):
        hidden_out[0, i, lon:lon_pad, :] = zero

    def head_step(t, carry):
        start = pl.multiple_of(t * tile, tile)
        for g in range(rows // 2):
            window = hs[pl.ds(start, tile + 2 * EDGE), 2 * g * ch : (2 * g + 4) * ch]
            fs[g, pl.ds(start, tile), :] = three_taps(window, w_head, (-1, 0, 1), tile)
        return carry

    lax.fori_loop(0, lon // tile, head_step, 0)
    pair = qp // (rows // 2)
    for g in range(rows // 2):
        fs[g, lon:lon_pad, :] = jnp.zeros((lon_pad - lon, fs.shape[2]), F32)
        fs[g, lon : lon + EDGE, :] = fs[g, 0:EDGE, :]
        fs[g, lon_pad - EDGE : lon_pad, :] = fs[g, lon - EDGE : lon, :]
        for j in range(pieces):
            turned = fs[g, j * piece : (j + 1) * piece, :].T
            field_out[j, 0, g * pair : (g + 1) * pair, :] = turned[:pair].astype(BF16)


def pair_kernel(dims, truth, rate, scale, *refs):
    members, taken, given, sub, piece = dims
    fields, outs, vals, accs = refs[:taken], refs[taken : taken + given], refs[-2], refs[-1]
    norm = 2.0 / (members - 1)
    pieces = fields[0].shape[0]
    for j in range(pieces):
        m = j * (members // pieces)
        for ref in fields:
            for k in range(ref.shape[1]):
                vals[m] = ref[j, k].astype(F32)
                m += 1
    blocks = piece // LANES

    def step(t, carry):
        r = pl.ds(pl.multiple_of((t // blocks) * 8, 8), 8)
        c = pl.ds(pl.multiple_of((t % blocks) * LANES, LANES), LANES)
        neg = rate[r, :]
        x = [vals[m, r, c] for m in range(members)]
        sums = [None] * members
        for i in range(members):
            for j in range(i + 1, members):
                d = x[j] - x[i]
                w = jnp.exp2(d * d * neg) * d
                sums[i] = w if sums[i] is None else sums[i] + w
                sums[j] = -w if sums[j] is None else sums[j] - w
        y = truth[r, c]
        sc = scale[r, :]
        for i in range(members):
            off = x[i] - y
            near = jnp.exp2(off * off * neg) * off
            accs[i, r, c] = sc * (norm * sums[i] + 2.0 * near)
        return carry

    lax.fori_loop(0, (sub // 8) * blocks, step, 0)
    for j in range(pieces):
        m = j * (members // pieces)
        for ref in outs:
            for k in range(ref.shape[1]):
                ref[j, k] = accs[m].astype(BF16)
                m += 1


def backward_kernel(dims, own, top, bot, hidden, slope, feats, w_back, *refs):
    rows, lon, lon_pad, ch, vp, pieces, piece, low, span = dims
    back_out, sums_out, gs, fx, acc_in, acc_hd = refs[-6:]
    ext = (rows + 4) * vp
    step_m = pl.program_id(0)

    @pl.when(step_m == 0)
    def _():
        acc_in[...] = jnp.zeros_like(acc_in)
        acc_hd[...] = jnp.zeros_like(acc_hd)

    for j in range(pieces):
        cols = slice(j * piece, (j + 1) * piece)
        gs[1, 0 : 2 * vp, cols] = top[j, 0]
        gs[1, 2 * vp : ext - 2 * vp, cols] = own[j, 0]
        gs[1, ext - 2 * vp : ext, cols] = bot[j, 0]
    for t in range(ext // 16):
        r = slice(t * 16, (t + 1) * 16)
        block = gs[1, r, :].astype(F32)
        gs[0, r, :] = pltpu.roll(block, lon_pad - 1, 1).astype(BF16)
        gs[2, r, :] = pltpu.roll(block, 1, 1).astype(BF16)
    for r in range(rows):
        fx[EDGE : EDGE + lon, r * ch : (r + 1) * ch] = feats[0, r]
    wrap_edges(fx, lon)
    fx[lon + 2 * EDGE :] = jnp.zeros((lon_pad - lon, rows * ch), BF16)
    tile = tile_of(lon_pad, LANES, 512)

    def step(t, carry):
        start = pl.multiple_of(t * tile, tile)
        rows_back = []
        for p in range((rows + 2) // 2):
            patch = jnp.concatenate(
                [gs[b, 2 * p * vp : (2 * p + 4) * vp, pl.ds(start, tile)] for b in range(3)], axis=0
            )
            back = lax.dot_general(
                patch, w_back[...], (((0,), (0,)), ((), ())), preferred_element_type=F32
            )
            for k in range(2):
                i = 2 * p + k
                part = back[:, k * ch : (k + 1) * ch] * slope[0, i, pl.ds(start, tile), :].astype(F32)
                part = part.astype(BF16)
                back_out[0, i, pl.ds(start, tile), :] = part
                rows_back.append(part)
        for g in range(rows // 2):
            base = 2 * g * vp + low
            patch = jnp.concatenate(
                [gs[b, base : base + span, pl.ds(start, tile)] for b in range(3)], axis=0
            )
            act = jnp.concatenate(
                [hidden[0, 2 * g + k, pl.ds(start, tile), :] for k in range(2)], axis=1
            )
            acc_hd[...] += jnp.dot(patch, act, preferred_element_type=F32)
            window = fx[pl.ds(start, tile + 2 * EDGE), 2 * g * ch : (2 * g + 2) * ch].astype(F32)
            act = jnp.concatenate(
                [moved(window, off, tile).astype(BF16) for off in (-1, 0, 1)], axis=1
            )
            back = jnp.concatenate(rows_back[2 * g : 2 * g + 4], axis=1)
            acc_in[...] += lax.dot_general(
                act, back, (((0,), (0,)), ((), ())), preferred_element_type=F32
            )
        return carry

    lax.fori_loop(0, lon_pad // tile, step, 0)

    @pl.when(step_m == pl.num_programs(0) - 1)
    def _():
        for a in range(3):
            for b in range(3):
                inner = None
                head = None
                for k in range(2):
                    n = k + 2 - a
                    at = b * 2 * ch + k * ch
                    part = acc_in[at : at + ch, n * ch : (n + 1) * ch]
                    inner = part if inner is None else inner + part
                    n = k + 3 - a
                    at = b * span + n * vp - low
                    part = acc_hd[at : at + vp, k * ch : (k + 1) * ch]
                    head = part if head is None else head + part
                q = 3 * a + b
                sums_out[q * ch : (q + 1) * ch, :] = inner
                at = 9 * ch + q * vp
                sums_out[at : at + vp, :] = head


def feature_kernel(dims, back, w_grad, grad_out, bs):
    rows, lon, ch = dims
    for i in range(rows + 2):
        bs[EDGE : EDGE + lon, i * ch : (i + 1) * ch] = back[0, i, :lon]
    wrap_edges(bs, lon)
    tile = tile_of(lon, 16, TILE)

    def step(t, carry):
        start = pl.multiple_of(t * tile, tile)
        for g in range(rows // 2):
            window = bs[pl.ds(start, tile + 2 * EDGE), 2 * g * ch : (2 * g + 4) * ch]
            grad = three_taps(window, w_grad, (1, 0, -1), tile)
            for k in range(2):
                grad_out[0, 2 * g + k, pl.ds(start, tile), :] = grad[
                    :, k * ch : (k + 1) * ch
                ].astype(BF16)
        return carry

    lax.fori_loop(0, lon // tile, step, 0)


def forward_weights(kernel, width):
    ch, outs = kernel.shape[2], kernel.shape[3]
    kernel = jnp.pad(kernel, ((0, 0), (0, 0), (0, 0), (0, width - outs)))
    cols = []
    for out_row in range(2):
        taps = jnp.pad(kernel, ((out_row, 1 - out_row), (0, 0), (0, 0), (0, 0)))
        cols.append(jnp.moveaxis(taps, 0, 1))
    return jnp.stack(cols, axis=3).reshape(3, 4 * ch, 2 * width)


def backward_weights(kernel, width):
    ch, outs = kernel.shape[2], kernel.shape[3]
    kernel = jnp.pad(kernel, ((0, 0), (0, 0), (0, 0), (0, width - outs)))[::-1]
    cols = []
    for out_row in range(2):
        taps = jnp.pad(kernel, ((out_row, 1 - out_row), (0, 0), (0, 0), (0, 0)))
        cols.append(jnp.transpose(taps, (1, 0, 3, 2)))
    return jnp.stack(cols, axis=3).reshape(3, 4 * width, 2 * ch)


def groups_of(first, count, groups):
    out, end = [], first + count
    for g in range(min(groups, count)):
        size = -(-(end - first) // (min(groups, count) - g))
        out.append((first, size))
        first += size
    return out


def neighbours(tail, head, axis, skip=None):
    edges = [(i, i + 1) for i in range(lax.axis_size(axis) - 1) if i + 1 != skip]
    before = lax.ppermute(tail, axis, edges)
    after = lax.ppermute(head, axis, [(j, i) for i, j in edges])
    return before, after


def reduce_all(values, axes):
    count = math.prod(lax.axis_size(a) for a in axes)
    rows, width = values.shape
    part = -(-rows // (16 * count)) * 16
    padded = jnp.pad(values, ((0, part * count - rows), (0, 0))).astype(BF16)
    got = lax.all_to_all(padded, axes, 0, 0, tiled=True)
    summed = jnp.sum(got.reshape(count, part, width).astype(F32), axis=0).astype(BF16)
    spread = jnp.broadcast_to(summed[None], (count, part, width))
    full = lax.all_to_all(spread, axes, 0, 0)
    return full.reshape(count * part, width)[:rows].astype(F32)


def shards(features, conv_inner, conv_head, truth, kernel_width, var_weight):
    per, rows, lon, ch = features.shape
    variables = conv_head.shape[3]
    pieces = lax.axis_size("mem")
    members = per * pieces
    vp = -(-variables // 8) * 8
    qp = rows * vp
    piece = -(-lon // (LANES * pieces)) * LANES
    while lon + 2 * EDGE > piece * pieces:
        piece += LANES
    lon_pad = piece * pieces
    assert rows % 2 == 0 and lon % 16 == 0 and (2 * vp) % 16 == 0 and 2 * vp <= 256
    low = vp // 16 * 16
    span = -(-(5 * vp - low) // 16) * 16

    at = lax.axis_index("lat")
    count = lax.axis_size("lat")
    middle = count // 2
    flags = jnp.stack([at > 0, at < count - 1, at == middle, at == middle - 1]).astype(jnp.int32)

    w_inner = forward_weights(conv_inner, ch)
    w_head = jnp.pad(forward_weights(conv_head, vp), ((0, 0), (0, 0), (0, 256 - 2 * vp)))

    params = lambda mib: pltpu.CompilerParams(vmem_limit_bytes=mib * MIB)
    whole = lambda shape: pl.BlockSpec(shape, lambda m: (0,) * len(shape))
    member = lambda shape, base=0: pl.BlockSpec((1,) + shape, lambda m: (base + m,) + (0,) * len(shape))
    spread = lambda n: pl.BlockSpec((pieces, 1, n, piece), lambda m: (0, m, 0, 0))
    macs = 2 * lon * 12 * ch * 2 * ch

    kept_shapes = [
        jax.ShapeDtypeStruct((per, rows, lon_pad, ch), BF16),
        jax.ShapeDtypeStruct((per, rows + 2, lon_pad, ch), BF16),
    ]
    groups, behind = groups_of(0, per, len(AHEAD)), groups_of(0, per, BEHIND)
    calls = [groups_of(*group, parts) for group, parts in zip(groups, AHEAD)]

    def forward(first, count, group, top, bot, relayed, kept):
        field_shape = jax.ShapeDtypeStruct((pieces, group[1], qp, piece), BF16)
        dims = (rows, lon, lon_pad, ch, qp, pieces, piece)
        return pl.pallas_call(
            functools.partial(forward_kernel, dims + (len(relayed),)),
            grid=(count,),
            in_specs=[
                pl.BlockSpec(memory_space=pltpu.SMEM),
                member((rows, lon, ch), first),
                member((2, lon, ch)),
                member((2, lon, ch)),
                whole(w_inner.shape),
                whole(w_head.shape),
            ]
            + [member((2, lon, ch), first - groups[-1][0]) for _ in relayed]
            + [pl.BlockSpec(memory_space=pl.ANY)] * len(kept),
            out_specs=[
                member((rows, lon_pad, ch), first),
                member((rows + 2, lon_pad, ch), first),
                pl.BlockSpec((pieces, 1, qp, piece), lambda m: (0, first - group[0] + m, 0, 0)),
            ],
            out_shape=kept_shapes + [field_shape],
            input_output_aliases={6 + len(relayed) + k: k for k in range(len(kept))},
            scratch_shapes=[
                pltpu.VMEM((lon + 2 * EDGE, (rows + 4) * ch), BF16),
                pltpu.VMEM((lon + 2 * EDGE, (rows + 2) * ch), BF16),
                pltpu.VMEM((rows // 2, lon_pad, 256), F32),
            ],
            compiler_params=params(FWD_MIB),
            cost_estimate=pl.CostEstimate(
                flops=3 * macs * count, bytes_accessed=(6 << 20) * count, transcendentals=0
            ),
            name="forward",
        )(flags, features, top, bot, w_inner, w_head, *relayed, *kept)

    start, size = groups[-1]
    mine = features[start : start + size]
    edge = mine
    if rows > 2:
        edge = jnp.where(at == middle, mine[:, :2], mine[:, rows - 2 :])
    half = lax.ppermute(edge, "lat", [(middle - 1, count - 1), (middle, 0)])
    relayed = lax.ppermute(half, "lat", [(count - 1, middle), (0, middle - 1)])
    halos = []
    for first, number in sum(calls, []):
        mine = features[first : first + number]
        skip = middle if first >= start else None
        halos.append(neighbours(mine[:, rows - 2 :], mine[:, :2], "lat", skip))

    kept, traded, called = [], [], 0
    for group, parts in zip(groups, calls):
        field = []
        for first, number in parts:
            *kept, field = forward(
                first,
                number,
                group,
                *halos[called],
                [relayed] if first >= start else [],
                [*kept[:2], *field],
            )
            called, field = called + 1, [field]
        traded.append(lax.all_to_all(field[0], "mem", 0, 0, tiled=True))

    conv_inner, conv_head, truth, kernel_width, var_weight, _ = lax.optimization_barrier(
        (conv_inner, conv_head, truth, kernel_width, var_weight, field[0])
    )
    w_back = backward_weights(conv_head, vp).reshape(12 * vp, 2 * ch)
    w_grad = backward_weights(conv_inner, ch)
    truth_rows = jnp.moveaxis(truth, 1, 0)
    truth_rows = jnp.pad(truth_rows, ((0, 0), (0, vp - variables), (0, 0))).reshape(qp, lon)
    blank = jnp.zeros((qp, lon_pad - lon - 2 * EDGE), F32)
    truth_rows = jnp.concatenate(
        [truth_rows, truth_rows[:, :EDGE], blank, truth_rows[:, lon - EDGE :]], axis=1
    )
    truth_piece = lax.dynamic_slice_in_dim(truth_rows, lax.axis_index("mem") * piece, piece, 1)
    inverse = 1.0 / (kernel_width * kernel_width)
    spread_param = lambda v: jnp.broadcast_to(
        jnp.tile(jnp.pad(v, (0, vp - variables)), rows)[:, None], (qp, LANES)
    )
    rate = spread_param((-0.5 * math.log2(math.e)) * inverse)
    scale = spread_param(var_weight * inverse)
    sub = 16
    row_block = lambda width: pl.BlockSpec((sub, width), lambda i: (i, 0))
    field_block = lambda count: pl.BlockSpec((pieces, count, sub, piece), lambda i: (0, 0, i, 0))
    gradient = pl.pallas_call(
        functools.partial(pair_kernel, (members, len(groups), len(behind), sub, piece)),
        grid=(qp // sub,),
        in_specs=[row_block(piece), row_block(LANES), row_block(LANES)]
        + [field_block(count) for _, count in groups],
        out_specs=[field_block(count) for _, count in behind],
        out_shape=[
            jax.ShapeDtypeStruct((pieces, count, qp, piece), BF16) for _, count in behind
        ],
        scratch_shapes=[pltpu.VMEM((members, sub, piece), F32)] * 2,
        compiler_params=params(PAIR_MIB),
        cost_estimate=pl.CostEstimate(
            flops=4 * members * members * qp * piece,
            bytes_accessed=4 * members * qp * piece,
            transcendentals=members * members // 2 * qp * piece,
        ),
        name="pairs",
    )(truth_piece, rate, scale, *traded)

    sums_rows = 9 * (ch + vp)

    def backward(own, first, count, back):
        g_top, g_bot = neighbours(own[:, :, qp - 2 * vp :], own[:, :, : 2 * vp], "lat")
        return pl.pallas_call(
            functools.partial(
                backward_kernel, (rows, lon, lon_pad, ch, vp, pieces, piece, low, span)
            ),
            grid=(count,),
            in_specs=[
                spread(qp),
                spread(2 * vp),
                spread(2 * vp),
                member((rows, lon_pad, ch), first),
                member((rows + 2, lon_pad, ch), first),
                member((rows, lon, ch), first),
                whole(w_back.shape),
            ]
            + [pl.BlockSpec(memory_space=pl.ANY)] * len(back),
            out_specs=[member((rows + 2, lon_pad, ch), first), whole((sums_rows, ch))],
            out_shape=[kept_shapes[1], jax.ShapeDtypeStruct((sums_rows, ch), F32)],
            input_output_aliases={7 + k: k for k in range(len(back))},
            scratch_shapes=[
                pltpu.VMEM((3, (rows + 4) * vp, lon_pad), BF16),
                pltpu.VMEM((lon_pad + 2 * EDGE, rows * ch), BF16),
                pltpu.VMEM((6 * ch, 4 * ch), F32),
                pltpu.VMEM((3 * span, 2 * ch), F32),
            ],
            compiler_params=params(BACK_MIB),
            cost_estimate=pl.CostEstimate(
                flops=4 * macs * count, bytes_accessed=(6 << 20) * count, transcendentals=0
            ),
            name="backward",
        )(own, g_top, g_bot, *kept, features, w_back, *back)

    owned, back, sums = [], [], None
    for g in gradient:
        owned.append(lax.all_to_all(g, "mem", 0, 0, tiled=True))
    for own, chunk in zip(owned, behind):
        *back, part = backward(own, *chunk, back)
        sums = part if sums is None else sums + part
    grad_features = pl.pallas_call(
        functools.partial(feature_kernel, (rows, lon, ch)),
        grid=(per,),
        in_specs=[member((rows + 2, lon_pad, ch)), whole(w_grad.shape)],
        out_specs=member((rows, lon, ch)),
        out_shape=jax.ShapeDtypeStruct(features.shape, BF16),
        scratch_shapes=[pltpu.VMEM((lon + 2 * EDGE, (rows + 2) * ch), BF16)],
        compiler_params=params(LAST_MIB),
        cost_estimate=pl.CostEstimate(
            flops=macs * per, bytes_accessed=(4 << 20) * per, transcendentals=0
        ),
        name="features",
    )(*back, w_grad)

    total = reduce_all(sums, ("mem", "lat"))
    points = rows * lax.axis_size("lat") * lon
    inner_sum = total[: 9 * ch].reshape(3, 3, ch, ch)
    head_sum = total[9 * ch :].reshape(3, 3, vp, ch)[:, :, :variables]
    return (grad_features, inner_sum / points, jnp.swapaxes(head_sum, 2, 3) / points)


def solution(mesh):
    in_specs = (P("mem", "lat", None, None), P(), P(), P(None, "lat", None), P(), P())
    out_specs = (P("mem", "lat", None, None), P(), P())

    return jax.shard_map(shards, mesh=mesh, in_specs=in_specs, out_specs=out_specs, check_vma=False)
```

```python
import functools
import math

import jax
import jax.numpy as jnp
from jax import lax
from jax.experimental import pallas as pl
from jax.experimental.pallas import tpu as pltpu
from jax.sharding import PartitionSpec as P


BF16 = jnp.bfloat16
F32 = jnp.float32
LANES = 128
EDGE = 16
MIB = 1024 * 1024
FWD_MIB, PAIR_MIB, BACK_MIB, LAST_MIB = 60, 44, 44, 56
TILE = 1440
AHEAD = (2, 1)
BEHIND = 2


def tile_of(count, step, most):
    return max(t for t in range(step, most + 1, step) if count % t == 0)


def wrap_edges(ref, lon):
    ref[0:EDGE] = ref[lon : lon + EDGE]
    ref[lon + EDGE : lon + 2 * EDGE] = ref[EDGE : 2 * EDGE]


def moved(values, offset, tile):
    if offset:
        values = pltpu.roll(values, (-offset) % values.shape[0], 0)
    return values[EDGE : EDGE + tile]


def three_taps(window, weights, offsets, tile):
    total = None
    for b, offset in enumerate(offsets):
        part = jnp.dot(window, weights[b], preferred_element_type=F32)
        part = moved(part, offset, tile)
        total = part if total is None else total + part
    return total


def fill_taps(out, kernel, width):
    ch, outs = kernel.shape[2], kernel.shape[3]
    out[...] = jnp.zeros_like(out)
    for row in range(2):
        for a in range(3):
            for b in range(3):
                at = (row + a) * ch
                out[b, at : at + ch, row * width : row * width + outs] = kernel[a, b]


def forward_kernel(dims, flags, own, top, bot, conv_inner, conv_head, *refs):
    rows, lon, lon_pad, ch, qp, pieces, piece, relay = dims
    relayed = refs[0] if relay else None
    hidden_out, slope_out, field_out, xs, hs, fs, w_inner, w_head = refs[-8:]
    tile = tile_of(lon, 16, TILE)
    half = math.sqrt(2.0 / math.pi)

    @pl.when(pl.program_id(0) == 0)
    def _():
        fill_taps(w_inner, conv_inner, ch)
        fill_taps(w_head, conv_head, qp // rows)

    for j in range(rows + 4):
        if j < 2:
            row = top[0, j]
            if relayed is not None:
                row = jnp.where(flags[2] != 0, relayed[0, j], row)
        elif j < rows + 2:
            row = own[0, j - 2]
        else:
            row = bot[0, j - rows - 2]
            if relayed is not None:
                row = jnp.where(flags[3] != 0, relayed[0, j - rows - 2], row)
        xs[EDGE : EDGE + lon, j * ch : (j + 1) * ch] = row
    wrap_edges(xs, lon)
    top_ok = flags[0].astype(F32)
    bot_ok = flags[1].astype(F32)

    def inner_step(t, carry):
        start = pl.multiple_of(t * tile, tile)
        for p in range((rows + 2) // 2):
            window = xs[pl.ds(start, tile + 2 * EDGE), 2 * p * ch : (2 * p + 4) * ch]
            pre = three_taps(window, w_inner, (-1, 0, 1), tile)
            square = pre * pre
            tanh = jnp.tanh(pre * (half + (half * 0.044715) * square))
            upper = 0.5 + 0.5 * tanh
            hidden = pre * upper
            slope = upper + hidden * (1.0 - upper) * (2.0 * half + (6.0 * half * 0.044715) * square)
            for k in range(2):
                i = 2 * p + k
                h = hidden[:, k * ch : (k + 1) * ch]
                s = slope[:, k * ch : (k + 1) * ch]
                if i == 0:
                    h, s = h * top_ok, s * top_ok
                if i == rows + 1:
                    h, s = h * bot_ok, s * bot_ok
                h = h.astype(BF16)
                hs[pl.ds(start + EDGE, tile), i * ch : (i + 1) * ch] = h
                slope_out[0, i, pl.ds(start, tile), :] = s.astype(BF16)
                if 1 <= i <= rows:
                    hidden_out[0, i - 1, pl.ds(start, tile), :] = h
        return carry

    lax.fori_loop(0, lon // tile, inner_step, 0)
    wrap_edges(hs, lon)
    zero = jnp.zeros((lon_pad - lon, ch), BF16)
    for i in range(rows + 2):
        slope_out[0, i, lon:lon_pad, :] = zero
    for i in range(rows):
        hidden_out[0, i, lon:lon_pad, :] = zero

    def head_step(t, carry):
        start = pl.multiple_of(t * tile, tile)
        for g in range(rows // 2):
            window = hs[pl.ds(start, tile + 2 * EDGE), 2 * g * ch : (2 * g + 4) * ch]
            fs[g, pl.ds(start, tile), :] = three_taps(window, w_head, (-1, 0, 1), tile)
        return carry

    lax.fori_loop(0, lon // tile, head_step, 0)
    pair = qp // (rows // 2)
    for g in range(rows // 2):
        fs[g, lon:lon_pad, :] = jnp.zeros((lon_pad - lon, fs.shape[2]), F32)
        fs[g, lon : lon + EDGE, :] = fs[g, 0:EDGE, :]
        fs[g, lon_pad - EDGE : lon_pad, :] = fs[g, lon - EDGE : lon, :]
        for j in range(pieces):
            turned = fs[g, j * piece : (j + 1) * piece, :].astype(BF16).T
            field_out[j, 0, g * pair : (g + 1) * pair, :] = turned[:pair]


def pair_kernel(dims, truth, rate, scale, *refs):
    members, taken, given, sub, piece = dims
    fields, outs, vals, accs = refs[:taken], refs[taken : taken + given], refs[-2], refs[-1]
    norm = 2.0 / (members - 1)
    pieces = fields[0].shape[0]
    for j in range(pieces):
        m = j * (members // pieces)
        for ref in fields:
            for k in range(ref.shape[1]):
                vals[m] = ref[j, k].astype(F32)
                m += 1
    blocks = piece // LANES

    def step(t, carry):
        r = pl.ds(pl.multiple_of((t // blocks) * 8, 8), 8)
        c = pl.ds(pl.multiple_of((t % blocks) * LANES, LANES), LANES)
        neg = rate[r, :]
        x = [vals[m, r, c] for m in range(members)]
        sums = [None] * members
        for i in range(members):
            for j in range(i + 1, members):
                d = x[j] - x[i]
                w = jnp.exp2(d * d * neg) * d
                sums[i] = w if sums[i] is None else sums[i] + w
                sums[j] = -w if sums[j] is None else sums[j] - w
        y = truth[r, c]
        sc = scale[r, :]
        for i in range(members):
            off = x[i] - y
            near = jnp.exp2(off * off * neg) * off
            accs[i, r, c] = sc * (norm * sums[i] + 2.0 * near)
        return carry

    lax.fori_loop(0, (sub // 8) * blocks, step, 0)
    for j in range(pieces):
        m = j * (members // pieces)
        for ref in outs:
            for k in range(ref.shape[1]):
                ref[j, k] = accs[m].astype(BF16)
                m += 1


def backward_kernel(dims, own, top, bot, hidden, slope, feats, w_back, *refs):
    rows, lon, lon_pad, ch, vp, outs, pieces, piece, low, span = dims
    back_out, sums_out, gs, fx, acc_in, acc_hd = refs[-6:]
    ext = (rows + 4) * vp
    step_m = pl.program_id(0)

    @pl.when(step_m == 0)
    def _():
        acc_in[...] = jnp.zeros_like(acc_in)
        acc_hd[...] = jnp.zeros_like(acc_hd)

    for j in range(pieces):
        cols = slice(j * piece, (j + 1) * piece)
        gs[1, 0 : 2 * vp, cols] = top[j, 0]
        gs[1, 2 * vp : ext - 2 * vp, cols] = own[j, 0]
        gs[1, ext - 2 * vp : ext, cols] = bot[j, 0]
    lane = lax.broadcasted_iota(jnp.int32, (16, LANES), 1)
    blocks = lon_pad // LANES
    for t in range(ext // 16):
        r = slice(t * 16, (t + 1) * 16)
        parts = [gs[1, r, j * LANES : (j + 1) * LANES].astype(F32) for j in range(blocks)]
        ahead = [pltpu.roll(part, LANES - 1, 1) for part in parts]
        behind = [pltpu.roll(part, 1, 1) for part in parts]
        for j in range(blocks):
            cols = slice(j * LANES, (j + 1) * LANES)
            after = ahead[(j + 1) % blocks]
            gs[0, r, cols] = jnp.where(lane == LANES - 1, after, ahead[j]).astype(BF16)
            gs[2, r, cols] = jnp.where(lane == 0, behind[j - 1], behind[j]).astype(BF16)
    for r in range(rows):
        fx[EDGE : EDGE + lon, r * ch : (r + 1) * ch] = feats[0, r]
    wrap_edges(fx, lon)
    fx[lon + 2 * EDGE :] = jnp.zeros((lon_pad - lon, rows * ch), BF16)
    tile = tile_of(lon_pad, LANES, 512)

    def step(t, carry):
        start = pl.multiple_of(t * tile, tile)
        rows_back = []
        for p in range((rows + 2) // 2):
            patch = jnp.concatenate(
                [gs[b, 2 * p * vp : (2 * p + 4) * vp, pl.ds(start, tile)] for b in range(3)], axis=0
            )
            back = lax.dot_general(
                patch, w_back[...], (((0,), (0,)), ((), ())), preferred_element_type=F32
            )
            for k in range(2):
                i = 2 * p + k
                part = back[:, k * ch : (k + 1) * ch] * slope[0, i, pl.ds(start, tile), :].astype(F32)
                part = part.astype(BF16)
                back_out[0, i, pl.ds(start, tile), :] = part
                rows_back.append(part)
        for g in range(rows // 2):
            base = 2 * g * vp + low
            patch = jnp.concatenate(
                [gs[b, base : base + span, pl.ds(start, tile)] for b in range(3)], axis=0
            )
            act = jnp.concatenate(
                [hidden[0, 2 * g + k, pl.ds(start, tile), :] for k in range(2)], axis=1
            )
            acc_hd[...] += jnp.dot(patch, act, preferred_element_type=F32)
            window = fx[pl.ds(start, tile + 2 * EDGE), 2 * g * ch : (2 * g + 2) * ch].astype(F32)
            act = jnp.concatenate(
                [moved(window, off, tile).astype(BF16) for off in (-1, 0, 1)], axis=1
            )
            back = jnp.concatenate(rows_back[2 * g : 2 * g + 4], axis=1)
            acc_in[...] += lax.dot_general(
                act, back, (((0,), (0,)), ((), ())), preferred_element_type=F32
            )
        return carry

    lax.fori_loop(0, lon_pad // tile, step, 0)

    @pl.when(step_m == pl.num_programs(0) - 1)
    def _():
        for a in range(3):
            for b in range(3):
                inner = None
                head = None
                for k in range(2):
                    n = k + 2 - a
                    at = b * 2 * ch + k * ch
                    part = acc_in[at : at + ch, n * ch : (n + 1) * ch]
                    inner = part if inner is None else inner + part
                    n = k + 3 - a
                    at = b * span + n * vp - low
                    part = acc_hd[at : at + vp, k * ch : (k + 1) * ch]
                    head = part if head is None else head + part
                q = 3 * a + b
                sums_out[q * ch : (q + 1) * ch, :] = inner
                at = 9 * ch + q * outs
                sums_out[at : at + outs, :] = head[:outs]


def feature_kernel(dims, back, w_grad, grad_out, bs):
    rows, lon, ch = dims
    for i in range(rows + 2):
        bs[EDGE : EDGE + lon, i * ch : (i + 1) * ch] = back[0, i, :lon]
    wrap_edges(bs, lon)
    tile = tile_of(lon, 16, TILE)

    def step(t, carry):
        start = pl.multiple_of(t * tile, tile)
        for g in range(rows // 2):
            window = bs[pl.ds(start, tile + 2 * EDGE), 2 * g * ch : (2 * g + 4) * ch]
            grad = three_taps(window, w_grad, (1, 0, -1), tile)
            for k in range(2):
                grad_out[0, 2 * g + k, pl.ds(start, tile), :] = grad[
                    :, k * ch : (k + 1) * ch
                ].astype(BF16)
        return carry

    lax.fori_loop(0, lon // tile, step, 0)


def backward_weights(kernel, width):
    ch, outs = kernel.shape[2], kernel.shape[3]
    kernel = jnp.pad(kernel, ((0, 0), (0, 0), (0, 0), (0, width - outs)))[::-1]
    cols = []
    for out_row in range(2):
        taps = jnp.pad(kernel, ((out_row, 1 - out_row), (0, 0), (0, 0), (0, 0)))
        cols.append(jnp.transpose(taps, (1, 0, 3, 2)))
    return jnp.stack(cols, axis=3).reshape(3, 4 * width, 2 * ch)


def groups_of(first, count, groups):
    out, end = [], first + count
    for g in range(min(groups, count)):
        size = -(-(end - first) // (min(groups, count) - g))
        out.append((first, size))
        first += size
    return out


def neighbours(tail, head, axis, skip=None):
    edges = [(i, i + 1) for i in range(lax.axis_size(axis) - 1) if i + 1 != skip]
    before = lax.ppermute(tail, axis, edges)
    after = lax.ppermute(head, axis, [(j, i) for i, j in edges])
    return before, after


def reduce_all(values, axes):
    count = math.prod(lax.axis_size(a) for a in axes)
    rows, width = values.shape
    part = -(-rows // (8 * count)) * 8
    padded = jnp.pad(values, ((0, part * count - rows), (0, 0))).astype(BF16)
    got = lax.all_to_all(padded, axes, 0, 0, tiled=True)
    summed = jnp.sum(got.reshape(count, part, width).astype(F32), axis=0).astype(BF16)
    spread = jnp.broadcast_to(summed[None], (count, part, width))
    full = lax.all_to_all(spread, axes, 0, 0)
    return full.reshape(count * part, width)[:rows].astype(F32)


def shards(features, conv_inner, conv_head, truth, kernel_width, var_weight):
    per, rows, lon, ch = features.shape
    variables = conv_head.shape[3]
    pieces = lax.axis_size("mem")
    members = per * pieces
    vp = -(-variables // 8) * 8
    qp = rows * vp
    piece = -(-lon // (LANES * pieces)) * LANES
    while lon + 2 * EDGE > piece * pieces:
        piece += LANES
    lon_pad = piece * pieces
    assert rows % 2 == 0 and lon % 16 == 0 and (2 * vp) % 16 == 0 and 2 * vp <= 256
    low = vp // 16 * 16
    span = -(-(5 * vp - low) // 16) * 16

    at = lax.axis_index("lat")
    count = lax.axis_size("lat")
    middle = count // 2
    flags = jnp.stack([at > 0, at < count - 1, at == middle, at == middle - 1]).astype(jnp.int32)

    params = lambda mib: pltpu.CompilerParams(vmem_limit_bytes=mib * MIB)
    whole = lambda shape: pl.BlockSpec(shape, lambda m: (0,) * len(shape))
    member = lambda shape, base=0: pl.BlockSpec((1,) + shape, lambda m: (base + m,) + (0,) * len(shape))
    spread = lambda n: pl.BlockSpec((pieces, 1, n, piece), lambda m: (0, m, 0, 0))
    macs = 2 * lon * 12 * ch * 2 * ch

    kept_shapes = [
        jax.ShapeDtypeStruct((per, rows, lon_pad, ch), BF16),
        jax.ShapeDtypeStruct((per, rows + 2, lon_pad, ch), BF16),
    ]
    groups, behind = groups_of(0, per, len(AHEAD)), groups_of(0, per, BEHIND)
    calls = [groups_of(*group, parts) for group, parts in zip(groups, AHEAD)]

    def forward(first, count, group, top, bot, relayed, kept):
        field_shape = jax.ShapeDtypeStruct((pieces, group[1], qp, piece), BF16)
        dims = (rows, lon, lon_pad, ch, qp, pieces, piece)
        return pl.pallas_call(
            functools.partial(forward_kernel, dims + (len(relayed),)),
            grid=(count,),
            in_specs=[
                pl.BlockSpec(memory_space=pltpu.SMEM),
                member((rows, lon, ch), first),
                member((2, lon, ch)),
                member((2, lon, ch)),
                whole(conv_inner.shape),
                whole(conv_head.shape),
            ]
            + [member((2, lon, ch), first - groups[-1][0]) for _ in relayed]
            + [pl.BlockSpec(memory_space=pl.ANY)] * len(kept),
            out_specs=[
                member((rows, lon_pad, ch), first),
                member((rows + 2, lon_pad, ch), first),
                pl.BlockSpec((pieces, 1, qp, piece), lambda m: (0, first - group[0] + m, 0, 0)),
            ],
            out_shape=kept_shapes + [field_shape],
            input_output_aliases={6 + len(relayed) + k: k for k in range(len(kept))},
            scratch_shapes=[
                pltpu.VMEM((lon + 2 * EDGE, (rows + 4) * ch), BF16),
                pltpu.VMEM((lon + 2 * EDGE, (rows + 2) * ch), BF16),
                pltpu.VMEM((rows // 2, lon_pad, 2 * LANES), F32),
                pltpu.VMEM((3, 4 * ch, 2 * ch), BF16),
                pltpu.VMEM((3, 4 * ch, 2 * LANES), BF16),
            ],
            compiler_params=params(FWD_MIB),
            cost_estimate=pl.CostEstimate(
                flops=3 * macs * count, bytes_accessed=(6 << 20) * count, transcendentals=0
            ),
            name="forward",
        )(flags, features, top, bot, conv_inner, conv_head, *relayed, *kept)

    start, size = groups[-1]
    mine = features[start : start + size]
    edge = mine
    if rows > 2:
        edge = jnp.where(at == middle, mine[:, :2], mine[:, rows - 2 :])
    half = lax.ppermute(edge, "lat", [(middle - 1, count - 1), (middle, 0)])
    relayed = lax.ppermute(half, "lat", [(count - 1, middle), (0, middle - 1)])
    halos = []
    for first, number in sum(calls, []):
        mine = features[first : first + number]
        skip = middle if first >= start else None
        halos.append(neighbours(mine[:, rows - 2 :], mine[:, :2], "lat", skip))

    kept, traded, called = [], [], 0
    for group, parts in zip(groups, calls):
        field = []
        for first, number in parts:
            *kept, field = forward(
                first,
                number,
                group,
                *halos[called],
                [relayed] if first >= start else [],
                [*kept[:2], *field],
            )
            called, field = called + 1, [field]
        traded.append(lax.all_to_all(field[0], "mem", 0, 0, tiled=True))

    inner, head, truth, kernel_width, var_weight, _ = lax.optimization_barrier(
        (conv_inner, conv_head, truth, kernel_width, var_weight, field[0])
    )
    w_back = backward_weights(head, vp).reshape(12 * vp, 2 * ch)
    w_grad = backward_weights(inner, ch)
    truth_rows = jnp.moveaxis(truth, 1, 0)
    truth_rows = jnp.pad(truth_rows, ((0, 0), (0, vp - variables), (0, 0))).reshape(qp, lon)
    blank = jnp.zeros((qp, lon_pad - lon - 2 * EDGE), F32)
    truth_rows = jnp.concatenate(
        [truth_rows, truth_rows[:, :EDGE], blank, truth_rows[:, lon - EDGE :]], axis=1
    )
    truth_piece = lax.dynamic_slice_in_dim(truth_rows, lax.axis_index("mem") * piece, piece, 1)
    inverse = 1.0 / (kernel_width * kernel_width)
    spread_param = lambda v: jnp.broadcast_to(
        jnp.tile(jnp.pad(v, (0, vp - variables)), rows)[:, None], (qp, LANES)
    )
    rate = spread_param((-0.5 * math.log2(math.e)) * inverse)
    scale = spread_param(var_weight * inverse)
    sub = 48 if qp % 48 == 0 else 16
    row_block = lambda width: pl.BlockSpec((sub, width), lambda i: (i, 0))
    field_block = lambda count: pl.BlockSpec((pieces, count, sub, piece), lambda i: (0, 0, i, 0))
    gradient = pl.pallas_call(
        functools.partial(pair_kernel, (members, len(groups), len(behind), sub, piece)),
        grid=(qp // sub,),
        in_specs=[row_block(piece), row_block(LANES), row_block(LANES)]
        + [field_block(count) for _, count in groups],
        out_specs=[field_block(count) for _, count in behind],
        out_shape=[
            jax.ShapeDtypeStruct((pieces, count, qp, piece), BF16) for _, count in behind
        ],
        scratch_shapes=[pltpu.VMEM((members, sub, piece), F32)] * 2,
        compiler_params=params(PAIR_MIB),
        cost_estimate=pl.CostEstimate(
            flops=4 * members * members * qp * piece,
            bytes_accessed=4 * members * qp * piece,
            transcendentals=members * members // 2 * qp * piece,
        ),
        name="pairs",
    )(truth_piece, rate, scale, *traded)

    sums_rows = 9 * (ch + variables)

    def backward(own, first, count, back):
        g_top, g_bot = neighbours(own[:, :, qp - 2 * vp :], own[:, :, : 2 * vp], "lat")
        return pl.pallas_call(
            functools.partial(
                backward_kernel, (rows, lon, lon_pad, ch, vp, variables, pieces, piece, low, span)
            ),
            grid=(count,),
            in_specs=[
                spread(qp),
                spread(2 * vp),
                spread(2 * vp),
                member((rows, lon_pad, ch), first),
                member((rows + 2, lon_pad, ch), first),
                member((rows, lon, ch), first),
                whole(w_back.shape),
            ]
            + [pl.BlockSpec(memory_space=pl.ANY)] * len(back),
            out_specs=[member((rows + 2, lon_pad, ch), first), whole((sums_rows, ch))],
            out_shape=[kept_shapes[1], jax.ShapeDtypeStruct((sums_rows, ch), F32)],
            input_output_aliases={7 + k: k for k in range(len(back))},
            scratch_shapes=[
                pltpu.VMEM((3, (rows + 4) * vp, lon_pad), BF16),
                pltpu.VMEM((lon_pad + 2 * EDGE, rows * ch), BF16),
                pltpu.VMEM((6 * ch, 4 * ch), F32),
                pltpu.VMEM((3 * span, 2 * ch), F32),
            ],
            compiler_params=params(BACK_MIB),
            cost_estimate=pl.CostEstimate(
                flops=4 * macs * count, bytes_accessed=(6 << 20) * count, transcendentals=0
            ),
            name="backward",
        )(own, g_top, g_bot, *kept, features, w_back, *back)

    owned, back, sums = [], [], None
    for g in gradient:
        owned.append(lax.all_to_all(g, "mem", 0, 0, tiled=True))
    for own, chunk in zip(owned, behind):
        *back, part = backward(own, *chunk, back)
        sums = part if sums is None else sums + part
    grad_features = pl.pallas_call(
        functools.partial(feature_kernel, (rows, lon, ch)),
        grid=(per,),
        in_specs=[member((rows + 2, lon_pad, ch)), whole(w_grad.shape)],
        out_specs=member((rows, lon, ch)),
        out_shape=jax.ShapeDtypeStruct(features.shape, BF16),
        scratch_shapes=[pltpu.VMEM((lon + 2 * EDGE, (rows + 2) * ch), BF16)],
        compiler_params=params(LAST_MIB),
        cost_estimate=pl.CostEstimate(
            flops=macs * per, bytes_accessed=(4 << 20) * per, transcendentals=0
        ),
        name="features",
    )(*back, w_grad)

    total = reduce_all(sums, ("mem", "lat"))
    points = rows * lax.axis_size("lat") * lon
    inner_sum = total[: 9 * ch].reshape(3, 3, ch, ch)
    head_sum = total[9 * ch :].reshape(3, 3, variables, ch)
    return (grad_features, inner_sum / points, jnp.swapaxes(head_sum, 2, 3) / points)


def solution(mesh):
    in_specs = (P("mem", "lat", None, None), P(), P(), P(None, "lat", None), P(), P())
    out_specs = (P("mem", "lat", None, None), P(), P())

    return jax.shard_map(shards, mesh=mesh, in_specs=in_specs, out_specs=out_specs, check_vma=False)
```
